32 devices in a mesh: cells: 8 (over y, x, core), obs: 4 (over z).
Axes of the slice: x: 2, y: 2, z: 4, core: 2. Of those that a mesh axis runs over, the one named last changes fastest.
Arguments:
- histories: bfloat16 [64, 384], P('obs'), may hold values from -6 to 6
- amplitude: bfloat16 [64, 5, 8192], P('obs', None, 'cells'), may hold values from -0.75 to 0.75
- weights: bfloat16 [8192, 256], P('cells'), may hold values from -0.375 to 0.375
- retarded: int32 [64, 64], P('obs', 'cells'), may hold values from 0 to 128
- owner_block: int32 [8192], P('cells'), may hold values from 0 to 7, as said below
- owner_cell: int32 [8192], P('cells'), may hold values from 0 to 16383
- adjoint: float32 [5, 16, 64, 128], P(None, 'cells', 'obs'), may hold values from -6 to 6
- step_size: float32 [16, 64, 128], P('cells', 'obs'), may hold values from 0.1 to 0.6
- jacobian: float32 [8, 3, 5, 5], P('cells'), may hold values from -6 to 6
Outputs:
- adjoint_next: float32 [5, 16, 64, 128], P(None, 'cells', 'obs')
- panel_source: float32 [5, 8192], P(None, 'cells')
The draws below stay inside these ranges and needn't reach their ends.
Inputs may be any that keep to these rules, and one draw needn't show every extreme that they name: `owner_block`: among each device's 1024 panels at most 512 name one owner block; one owner block, drawn from the seed, is named by exactly 512 panels of every device.
All inputs are finite; a program needn't handle non-finite values.
Results may differ from the reference program's by a relative error of at most 0.0003.
Values sent between devices are 32-bit elements; how exact they have to be, the bound alone decides.
A program may use at most 192 MiB of HBM per device.

```python
import math
import jax
import jax.numpy as jnp
from jax import lax

NOBS = 64
SAMPLES = 256
SPAN = 128
COMP = 5
TILE = 128
PAN_DEV = 1024
AZ_DEV = 2
NZ = 128
HIST = 384
CAP = 512
PANELS = 8192
TILES = 64
NA = 16
NR = 64
BLOCK_CELLS = 16384
N_CELLS = 8


def draw_owner_block(key, part):
    folded = jax.random.fold_in(key, 7)
    first_key, shift_key, order_key = jax.random.split(folded, 3)
    crowded = jax.random.randint(first_key, (), 0, N_CELLS)
    shifts = jax.random.randint(shift_key, (N_CELLS, 1), 0, N_CELLS - 1)
    within = jnp.arange(PAN_DEV, dtype=jnp.int32)[None, :]
    others = (crowded + 1 + (within - CAP + shifts) % (N_CELLS - 1)) % N_CELLS
    blocks = jnp.where(within < CAP, crowded, others)

    def shuffle(block_key):
        return jax.random.permutation(block_key, PAN_DEV)
    orders = jax.vmap(shuffle)(jax.random.split(order_key, N_CELLS))
    shuffled = jnp.take_along_axis(blocks, orders, axis=1)
    return shuffled.reshape(PANELS).astype(jnp.int32)


def plant(entries, rng, low, largest):
    place = [jax.random.randint(jax.random.fold_in(rng, axis), (), 0, length) for axis, length in enumerate(entries.shape)]
    widest = entries.shape.index(max(entries.shape))
    next_to = place[:widest] + [(place[widest] + 1) % entries.shape[widest]] + place[widest + 1:]
    return entries.at[tuple(place)].set(low).at[tuple(next_to)].set(largest)


def level_of(stream_key, extent, shards, smallest, top_value):
    factor_of, own = 1.0, jax.random.fold_in(stream_key, 6)
    for position, blocks in shards:
        steps = jnp.exp(jax.random.uniform(jax.random.fold_in(own, position), (blocks,), jnp.float32, smallest / len(shards), top_value / len(shards)))
        factor_of = factor_of * jnp.repeat(steps, extent[position] // blocks).reshape([-1 if axis == position else 1 for axis in range(len(extent))])
    return factor_of


def gaussian(rng, extent, spread, most, cuts=(), kind=jnp.bfloat16):
    factor_of = level_of(rng, extent, cuts, -0.22, 0.18) if cuts else 1.0
    entries = jax.random.normal(rng, extent, jnp.float32) * spread * factor_of
    return jnp.minimum(jnp.maximum(entries, -most), most).astype(kind)


def setup_inputs(seed: int = 0) -> dict:
    streams_of = jax.random.split(jax.random.key(seed), 10)
    histories = gaussian(streams_of[0], (NOBS, HIST), 1.0, 6.0, ((0, 4),))
    amplitude = gaussian(streams_of[1], (NOBS, COMP, PANELS), NOBS ** -0.5, 0.75, ((0, 4), (2, 8)))
    weights = gaussian(streams_of[2], (PANELS, SAMPLES), SAMPLES ** -0.5, 0.375, ((0, 8),))
    retarded = plant(jax.random.randint(streams_of[3], (NOBS, TILES), 0, SPAN + 1), jax.random.fold_in(streams_of[3], 1), 0, SPAN).astype(jnp.int32)
    owner_block = draw_owner_block(jax.random.fold_in(streams_of[9], 71), 0)
    owner_cell = plant(jax.random.randint(streams_of[5], (PANELS,), 0, BLOCK_CELLS), jax.random.fold_in(streams_of[5], 1), 0, BLOCK_CELLS - 1).astype(jnp.int32)
    adjoint = gaussian(streams_of[6], (COMP, NA, NR, NZ), 1.0, 6.0, ((1, 8), (2, 4)), jnp.float32)
    step_size = jnp.clip(jnp.exp(math.log(0.6) - 1.7917595 * jax.random.uniform(streams_of[7], (NA, NR, NZ), jnp.float32) ** level_of(streams_of[7], (NA, NR, NZ), ((0, 8), (1, 4)), -0.2, 0.2)), 0.1, 0.6)
    jacobian = gaussian(streams_of[8], (N_CELLS, 3, COMP, COMP), 0.45, 6.0, ((0, 8),), jnp.float32)
    return dict(histories=histories, amplitude=amplitude, weights=weights, retarded=retarded, owner_block=owner_block, owner_cell=owner_cell, adjoint=adjoint, step_size=step_size, jacobian=jacobian)


smoothing = 0.25


def slide(series, offset):
    return lax.dynamic_slice_in_dim(series, offset, SAMPLES)


def reference(histories, amplitude, weights, retarded, owner_block, owner_cell, adjoint, step_size, jacobian):
    tile_count = PANELS // TILE
    weights_tiled = weights.reshape(tile_count, TILE, SAMPLES)
    amplitude_tiled = amplitude.reshape(NOBS, COMP, tile_count, TILE)

    def one_tile(tile_index):
        offsets = lax.dynamic_index_in_dim(retarded, tile_index, 1, keepdims=False)
        window = jax.vmap(slide)(histories, offsets)
        tiled = lax.dynamic_index_in_dim(weights_tiled, tile_index, 0, keepdims=False)
        projected = jnp.dot(tiled, window.T, preferred_element_type=jnp.float32)
        amps = lax.dynamic_index_in_dim(amplitude_tiled, tile_index, 2, keepdims=False).astype(jnp.float32)
        return jnp.sum(amps * projected.T[:, None, :], axis=0)

    sources = lax.map(one_tile, jnp.arange(tile_count, dtype=jnp.int32))
    panel_source = jnp.transpose(sources, (1, 0, 2)).reshape(COMP, PANELS)
    flat_index = owner_block * BLOCK_CELLS + owner_cell
    surface = jnp.zeros((COMP, NA * NR * NZ), jnp.float32).at[:, flat_index].add(panel_source)
    surface = surface.reshape(COMP, NA, NR, NZ)

    def rotate(direction, difference):
        reshaped = difference.reshape(COMP, N_CELLS, AZ_DEV, NR, NZ)
        rotated = jnp.einsum('bkc,kbarz->cbarz', jacobian[:, direction], reshaped, precision=lax.Precision.HIGHEST)
        return rotated.reshape(COMP, NA, NR, NZ)

    radial_pad = jnp.pad(adjoint, ((0, 0), (0, 0), (1, 1), (0, 0)))
    axial_pad = jnp.pad(adjoint, ((0, 0), (0, 0), (0, 0), (1, 1)))
    neighbours = (
        (jnp.roll(adjoint, -1, axis=1), jnp.roll(adjoint, 1, axis=1)),
        (radial_pad[:, :, 2:], radial_pad[:, :, :-2]),
        (axial_pad[..., 2:], axial_pad[..., :-2]),
    )
    summed = jnp.zeros_like(adjoint)
    for direction in range(3):
        forward, backward = neighbours[direction]
        summed = summed + (0.5 * rotate(direction, forward - backward) + smoothing * (forward - 2.0 * adjoint + backward))
    adjoint_next = adjoint + step_size[None] * summed + surface
    return (adjoint_next, panel_source)
```

```python
import functools

import jax
import jax.numpy as jnp
from jax import lax
from jax.experimental import pallas as pl
from jax.experimental.pallas import tpu as pltpu
from jax.sharding import PartitionSpec as P

MESH = pl.DeviceIdType.MESH
SMOOTHING = 0.25
NT = (((1,), (1,)), ((), ()))


def div(x, d):
    if d & (d - 1) == 0:
        return lax.shift_right_logical(x, jnp.full_like(x, d.bit_length() - 1))
    return lax.div(x, jnp.full_like(x, d))


def mod(x, d):
    if d & (d - 1) == 0:
        return x & (d - 1)
    return lax.rem(x, jnp.full_like(x, d))


def partner(me, j, n):
    if n & (n - 1):
        return lax.rem(me + j, n)
    out = me
    for k in range(n.bit_length() - 1):
        if j >> k & 1:
            out = out + (1 - 2 * ((me // (1 << k)) % 2)) * (1 << k)
    return out


def kernel(
    nc, no,
    hist_h, amp_h, wts_h, ret_h, ob_h, oc_h, adj_h, step_h, jac_h,
    out_ref, ps_ref,
    hist, amp, wts, ret, ob, oc, adj, step, jac,
    part, src, tgt, halo_a, halo_r, a_buf, bt, acc,
    in_sem, ps_send, ps_recv, s_send, s_recv, t_send, t_recv, h_send, h_recv,
):
    me, g = lax.axis_index("cells"), lax.axis_index("obs")
    loads = [
        pltpu.make_async_copy(h, v, in_sem.at[i])
        for i, (h, v) in enumerate(
            [(hist_h, hist), (ret_h, ret), (ob_h, ob), (oc_h, oc), (wts_h, wts), (amp_h, amp),
             (adj_h, adj), (step_h, step), (jac_h, jac)]
        )
    ]
    for c in loads:
        c.start()
    barrier = pltpu.get_barrier_semaphore()
    peers_c = [partner(me, j, nc) for j in range(nc)]
    peers_o = [lax.rem(g + k, no) for k in range(no)]
    for j in range(1, nc):
        pl.semaphore_signal(barrier, inc=1, device_id=(peers_c[j], g), device_id_type=MESH)
    for k in range(1, no):
        pl.semaphore_signal(barrier, inc=1, device_id=(me, peers_o[k]), device_id_type=MESH)

    nobs, comp = amp.shape[0], amp.shape[1]
    samples = wts.shape[1]
    hlen = hist.shape[1]
    tiles = ret.shape[1]
    tile = wts.shape[0] // tiles
    az, rl, nz = adj.shape[1:]
    radial_all = rl * no
    block_cells = az * radial_all * nz

    loads[0].wait()
    loads[1].wait()
    loads[2].wait()
    loads[3].wait()
    tgt[0] = ob[...] * block_cells + oc[...]
    series = hist[...].astype(jnp.float32)
    offsets = ret[...]
    span = hlen - samples
    windows = []
    for t in range(tiles):
        off = offsets[:, t : t + 1]
        x = series
        for bit in reversed(range(span.bit_length())):
            amount = 1 << bit
            moved = pltpu.roll(x, hlen - amount, 1)
            x = jnp.where((off >> bit & 1) == 1, moved, x)
        windows.append(x[:, :samples].astype(jnp.bfloat16))
    loads[4].wait()
    loads[5].wait()
    for t in range(tiles):
        cols = slice(t * tile, (t + 1) * tile)
        proj = lax.dot_general(windows[t], wts[cols, :], NT, preferred_element_type=jnp.float32)
        total = jnp.zeros((comp, tile), jnp.float32)
        for o in range(nobs):
            total = total + amp[o, :, cols].astype(jnp.float32) * proj[o : o + 1, :]
        for c in range(comp):
            part[g, c, t : t + 1, :] = total[c : c + 1, :]
    loads[6].wait()
    loads[7].wait()
    loads[8].wait()

    pl.semaphore_wait(barrier, nc - 1 + no - 1)

    def remote(s, d, ss, rs, dev):
        return pltpu.make_async_remote_copy(
            src_ref=s, dst_ref=d, send_sem=ss, recv_sem=rs, device_id=dev, device_id_type=MESH
        )

    part_copies = [
        remote(part.at[g], part.at[g], ps_send.at[k], ps_recv.at[k], (me, peers_o[k]))
        for k in range(1, no)
    ]
    for c in part_copies:
        c.start()
    tgt_copies = [
        remote(tgt.at[0], tgt.at[j], t_send.at[j], t_recv.at[j], (peers_c[j], g))
        for j in range(1, nc)
    ]
    for c in tgt_copies:
        c.start()
    after, before = lax.rem(me + 1, nc), lax.rem(me + nc - 1, nc)
    az_copies = [
        remote(adj.at[:, az - 1], halo_a.at[0], h_send.at[0], h_recv.at[0], (after, g)),
        remote(adj.at[:, 0], halo_a.at[1], h_send.at[1], h_recv.at[1], (before, g)),
    ]
    for c in az_copies:
        c.start()
    g_after, g_before = lax.rem(g + 1, no), lax.rem(g + no - 1, no)
    up = remote(adj.at[:, :, pl.ds(rl - 8, 8)], halo_r.at[0], h_send.at[2], h_recv.at[2], (me, g_after))
    down = remote(adj.at[:, :, pl.ds(0, 8)], halo_r.at[1], h_send.at[3], h_recv.at[3], (me, g_before))
    has_after, has_before = g < no - 1, g > 0

    @pl.when(has_after)
    def _():
        up.start()

    @pl.when(has_before)
    def _():
        down.start()

    column_id = lax.broadcasted_iota(jnp.int32, (az * nz, tile), 0) + me * (az * nz)
    row_id = lax.broadcasted_iota(jnp.int32, (rl, tile), 0) + g * rl

    def build_columns(j, slot):
        flat = tgt[j]
        code = div(flat, radial_all * nz) * nz + mod(flat, nz)
        for t in range(tiles):
            hit = code[t : t + 1, :] == column_id
            bt[slot, :, t * tile : (t + 1) * tile] = jnp.where(hit, 1.0, 0.0).astype(jnp.bfloat16)

    few = bt.shape[0] == nc
    if few:
        build_columns(0, 0)

    for c in az_copies:
        c.wait_recv()

    @pl.when(has_before)
    def _():
        up.wait_recv()

    @pl.when(has_after)
    def _():
        down.wait_recv()

    @pl.when(jnp.logical_not(has_before))
    def _():
        halo_r[0] = jnp.zeros(halo_r.shape[1:], jnp.float32)

    @pl.when(jnp.logical_not(has_after))
    def _():
        halo_r[1] = jnp.zeros(halo_r.shape[1:], jnp.float32)

    row = lax.broadcasted_iota(jnp.int32, (rl, nz), 0)
    lane = lax.broadcasted_iota(jnp.int32, (rl, nz), 1)
    for a in range(az):
        diffs = [[], [], []]
        sums = []
        for c in range(comp):
            x = adj[c, a]
            f0 = adj[c, a + 1] if a + 1 < az else halo_a[1, c]
            b0 = adj[c, a - 1] if a > 0 else halo_a[0, c]
            f1 = jnp.where(row == rl - 1, halo_r[1, c, a, 0:1, :], pltpu.roll(x, rl - 1, 0))
            b1 = jnp.where(row == 0, halo_r[0, c, a, 7:8, :], pltpu.roll(x, 1, 0))
            f2 = jnp.where(lane == nz - 1, 0.0, pltpu.roll(x, nz - 1, 1))
            b2 = jnp.where(lane == 0, 0.0, pltpu.roll(x, 1, 1))
            diffs[0].append(f0 - b0)
            diffs[1].append(f1 - b1)
            diffs[2].append(f2 - b2)
            sums.append(((f0 + b0) + (f1 + b1)) + (f2 + b2) - 6.0 * x)
        for c in range(comp):
            turned = jnp.zeros((rl, nz), jnp.float32)
            for d in range(3):
                for k in range(comp):
                    turned = turned + jac[0, d, k : k + 1, c : c + 1] * diffs[d][k]
            out_ref[c, a] = adj[c, a] + step[a] * (0.5 * turned + SMOOTHING * sums[c])

    if few:
        for j in range(1, nc):
            tgt_copies[j - 1].wait_recv()
            build_columns(j, j)

    for c in part_copies:
        c.wait_recv()
    total = part[0]
    for k in range(1, no):
        total = total + part[k]
    src[0] = total
    ps_ref[...] = total
    src_copies = [
        remote(src.at[0], src.at[j], s_send.at[j], s_recv.at[j], (peers_c[j], g))
        for j in range(1, nc)
    ]
    for c in src_copies:
        c.start()

    def land(j, slot, first):
        rad = mod(div(tgt[j], nz), radial_all)
        hits = [rad[t : t + 1, :] == row_id for t in range(tiles)]
        for c in range(comp):
            value = src[j, c]
            high = value.astype(jnp.bfloat16).astype(jnp.float32)
            for p, piece in enumerate((high, value - high)):
                top = (p * comp + c) * rl
                for t in range(tiles):
                    a_buf[slot, top : top + rl, t * tile : (t + 1) * tile] = jnp.where(
                        hits[t], piece[t : t + 1, :], 0.0
                    ).astype(jnp.bfloat16)
        got = lax.dot_general(
            a_buf[slot], bt[j if few else 0], NT, preferred_element_type=jnp.float32
        )
        got = got[: comp * rl] + got[comp * rl :]
        if first:
            acc[...] = got
        else:
            acc[...] += got

    if few:
        land(0, 0, True)
        for j in range(1, nc):
            src_copies[j - 1].wait_recv()
            land(j, j % 2, False)
    else:
        build_columns(0, 0)
        land(0, 0, True)

        def one(j, carry):
            remote(tgt.at[0], tgt.at[j], t_send.at[j], t_recv.at[j], (me, g)).wait_recv()
            remote(src.at[0], src.at[j], s_send.at[j], s_recv.at[j], (me, g)).wait_recv()
            build_columns(j, 0)
            land(j, 0, False)
            return carry

        lax.fori_loop(1, nc, one, 0)

    for c in range(comp):
        for a in range(az):
            out_ref[c, a] += acc[c * rl : (c + 1) * rl, a * nz : (a + 1) * nz]

    for c in part_copies + tgt_copies + az_copies + src_copies:
        c.wait_send()

    @pl.when(has_after)
    def _():
        up.wait_send()

    @pl.when(has_before)
    def _():
        down.wait_send()


def on_device(
    nc, no, histories, amplitude, weights, retarded, owner_block, owner_cell, adjoint, step_size, jacobian
):
    tiles = retarded.shape[1]
    tile = weights.shape[0] // tiles
    comp, az, rl, nz = adjoint.shape
    ob = owner_block.reshape(tiles, tile)
    oc = owner_cell.reshape(tiles, tile)
    args = (histories, amplitude, weights, retarded, ob, oc, adjoint, step_size, jacobian)
    slots = nc if nc <= 16 else 1
    f32 = jnp.float32
    dma = pltpu.SemaphoreType.DMA
    out, ps = pl.pallas_call(
        functools.partial(kernel, nc, no),
        out_shape=(
            jax.ShapeDtypeStruct(adjoint.shape, f32),
            jax.ShapeDtypeStruct((comp, tiles, tile), f32),
        ),
        in_specs=[pl.BlockSpec(memory_space=pl.ANY)] * len(args),
        out_specs=(pl.BlockSpec(memory_space=pltpu.VMEM),) * 2,
        scratch_shapes=[pltpu.VMEM(x.shape, x.dtype) for x in args]
        + [
            pltpu.VMEM((no, comp, tiles, tile), f32),
            pltpu.VMEM((nc, comp, tiles, tile), f32),
            pltpu.VMEM((nc, tiles, tile), jnp.int32),
            pltpu.VMEM((2, comp, rl, nz), f32),
            pltpu.VMEM((2, comp, az, 8, nz), f32),
            pltpu.VMEM((2, 2 * comp * rl, tiles * tile), jnp.bfloat16),
            pltpu.VMEM((slots, az * nz, tiles * tile), jnp.bfloat16),
            pltpu.VMEM((comp * rl, az * nz), f32),
            dma((len(args),)),
            dma((no,)),
            dma((no,)),
            dma((nc,)),
            dma((nc,)),
            dma((nc,)),
            dma((nc,)),
            dma((4,)),
            dma((4,)),
        ],
        compiler_params=pltpu.CompilerParams(
            collective_id=0, has_side_effects=True, vmem_limit_bytes=48 * 1024 * 1024
        ),
        name="rotor_step",
    )(*args)
    return out, ps.reshape(comp, tiles * tile)


def solution(mesh):
    return jax.shard_map(
        functools.partial(on_device, mesh.shape["cells"], mesh.shape["obs"]),
        mesh=mesh,
        in_specs=(
            P("obs", None),
            P("obs", None, "cells"),
            P("cells", None),
            P("obs", "cells"),
            P("cells"),
            P("cells"),
            P(None, "cells", "obs", None),
            P("cells", "obs", None),
            P("cells", None, None, None),
        ),
        out_specs=(P(None, "cells", "obs", None), P(None, "cells")),
        check_vma=False,
    )
```

```python
import functools

import jax
import jax.numpy as jnp
from jax import lax
from jax.experimental import pallas as pl
from jax.experimental.pallas import tpu as pltpu
from jax.sharding import PartitionSpec as P

MESH = pl.DeviceIdType.MESH
SMOOTHING = 0.25
NT = (((1,), (1,)), ((), ()))


def div(x, d):
    if d & (d - 1) == 0:
        return lax.shift_right_logical(x, jnp.full_like(x, d.bit_length() - 1))
    return lax.div(x, jnp.full_like(x, d))


def mod(x, d):
    if d & (d - 1) == 0:
        return x & (d - 1)
    return lax.rem(x, jnp.full_like(x, d))


def partner(me, j, n):
    if n & (n - 1):
        return lax.rem(me + j, n)
    out = me
    for k in range(n.bit_length() - 1):
        if j >> k & 1:
            out = out + (1 - 2 * ((me // (1 << k)) % 2)) * (1 << k)
    return out


def kernel(
    nc, no,
    hist_h, amp_h, wts_h, ret_h, ob_h, oc_h, adj_h, step_h, jac_h,
    out_ref, ps_ref,
    hist, amp, wts, ret, ob, oc, adj, step, jac,
    part, src, tgt, halo_a, halo_r, a_buf, bt, acc,
    in_sem, ps_send, ps_recv, s_send, s_recv, t_send, t_recv, h_send, h_recv,
):
    me, g = lax.axis_index("cells"), lax.axis_index("obs")
    loads = [
        pltpu.make_async_copy(h, v, in_sem.at[i])
        for i, (h, v) in enumerate(
            [(hist_h, hist), (ret_h, ret), (ob_h, ob), (oc_h, oc), (wts_h, wts), (amp_h, amp),
             (adj_h, adj), (step_h, step), (jac_h, jac)]
        )
    ]
    for c in loads:
        c.start()
    barrier = pltpu.get_barrier_semaphore()
    peers_c = [partner(me, j, nc) for j in range(nc)]
    peers_o = [lax.rem(g + k, no) for k in range(no)]
    for j in range(1, nc):
        pl.semaphore_signal(barrier, inc=1, device_id=(peers_c[j], g), device_id_type=MESH)
    for k in range(1, no):
        pl.semaphore_signal(barrier, inc=1, device_id=(me, peers_o[k]), device_id_type=MESH)

    comp, nobs = amp.shape[0], amp.shape[1]
    samples = wts.shape[1]
    hlen = hist.shape[1]
    tiles = ret.shape[0]
    tile = wts.shape[0] // tiles
    az, rl, nz = adj.shape[1:]
    radial_all = rl * no
    block_cells = az * radial_all * nz

    loads[0].wait()
    loads[1].wait()
    loads[2].wait()
    loads[3].wait()
    tgt[0] = ob[...] * block_cells + oc[...]
    series = hist[...].astype(jnp.float32)
    same = lax.broadcasted_iota(jnp.int32, (nobs, nobs), 0) == lax.broadcasted_iota(
        jnp.int32, (nobs, nobs), 1
    )
    offsets = ret[...].astype(jnp.float32)
    span = hlen - samples
    windows = []
    for t in range(tiles):
        off = jnp.sum(jnp.where(same, offsets[t : t + 1, :], 0.0), axis=1, keepdims=True)
        off = off.astype(jnp.int32)
        x = series
        for bit in reversed(range(span.bit_length())):
            amount = 1 << bit
            moved = pltpu.roll(x, hlen - amount, 1)
            x = jnp.where((off >> bit & 1) == 1, moved, x)
        windows.append(x[:, :samples].astype(jnp.bfloat16))
    loads[4].wait()
    loads[5].wait()
    for t in range(tiles):
        cols = slice(t * tile, (t + 1) * tile)
        proj = lax.dot_general(windows[t], wts[cols, :], NT, preferred_element_type=jnp.float32)
        for c in range(comp):
            product = amp[c, :, cols].astype(jnp.float32) * proj
            part[g, c, t : t + 1, :] = jnp.sum(product, axis=0, keepdims=True)
    loads[6].wait()
    loads[7].wait()
    loads[8].wait()

    pl.semaphore_wait(barrier, nc - 1 + no - 1)

    def remote(s, d, ss, rs, dev):
        return pltpu.make_async_remote_copy(
            src_ref=s, dst_ref=d, send_sem=ss, recv_sem=rs, device_id=dev, device_id_type=MESH
        )

    part_copies = [
        remote(part.at[g], part.at[g], ps_send.at[k], ps_recv.at[k], (me, peers_o[k]))
        for k in range(1, no)
    ]
    for c in part_copies:
        c.start()
    tgt_copies = [
        remote(tgt.at[0], tgt.at[j], t_send.at[j], t_recv.at[j], (peers_c[j], g))
        for j in range(1, nc)
    ]
    for c in tgt_copies:
        c.start()
    after, before = lax.rem(me + 1, nc), lax.rem(me + nc - 1, nc)
    az_copies = [
        remote(adj.at[:, az - 1], halo_a.at[0], h_send.at[0], h_recv.at[0], (after, g)),
        remote(adj.at[:, 0], halo_a.at[1], h_send.at[1], h_recv.at[1], (before, g)),
    ]
    for c in az_copies:
        c.start()
    g_after, g_before = lax.rem(g + 1, no), lax.rem(g + no - 1, no)
    up = remote(adj.at[:, :, pl.ds(rl - 8, 8)], halo_r.at[0], h_send.at[2], h_recv.at[2], (me, g_after))
    down = remote(adj.at[:, :, pl.ds(0, 8)], halo_r.at[1], h_send.at[3], h_recv.at[3], (me, g_before))
    has_after, has_before = g < no - 1, g > 0

    @pl.when(has_after)
    def _():
        up.start()

    @pl.when(has_before)
    def _():
        down.start()

    column_id = lax.broadcasted_iota(jnp.int32, (az * nz, tile), 0) + me * (az * nz)
    row_id = lax.broadcasted_iota(jnp.int32, (rl, tile), 0) + g * rl

    def build_columns(j, slot):
        flat = tgt[j]
        code = div(flat, radial_all * nz) * nz + mod(flat, nz)
        for t in range(tiles):
            hit = code[t : t + 1, :] == column_id
            bt[slot, :, t * tile : (t + 1) * tile] = jnp.where(hit, 1.0, 0.0).astype(jnp.bfloat16)

    few = bt.shape[0] == nc
    if few:
        build_columns(0, 0)

    for c in az_copies:
        c.wait_recv()

    @pl.when(has_before)
    def _():
        up.wait_recv()

    @pl.when(has_after)
    def _():
        down.wait_recv()

    @pl.when(jnp.logical_not(has_before))
    def _():
        halo_r[0] = jnp.zeros(halo_r.shape[1:], jnp.float32)

    @pl.when(jnp.logical_not(has_after))
    def _():
        halo_r[1] = jnp.zeros(halo_r.shape[1:], jnp.float32)

    row = lax.broadcasted_iota(jnp.int32, (rl, nz), 0)
    lane = lax.broadcasted_iota(jnp.int32, (rl, nz), 1)
    for a in range(az):
        diffs = [[], [], []]
        sums = []
        for c in range(comp):
            x = adj[c, a]
            f0 = adj[c, a + 1] if a + 1 < az else halo_a[1, c]
            b0 = adj[c, a - 1] if a > 0 else halo_a[0, c]
            f1 = jnp.where(row == rl - 1, halo_r[1, c, a, 0:1, :], pltpu.roll(x, rl - 1, 0))
            b1 = jnp.where(row == 0, halo_r[0, c, a, 7:8, :], pltpu.roll(x, 1, 0))
            f2 = jnp.where(lane == nz - 1, 0.0, pltpu.roll(x, nz - 1, 1))
            b2 = jnp.where(lane == 0, 0.0, pltpu.roll(x, 1, 1))
            diffs[0].append(f0 - b0)
            diffs[1].append(f1 - b1)
            diffs[2].append(f2 - b2)
            sums.append(((f0 + b0) + (f1 + b1)) + (f2 + b2) - 6.0 * x)
        for c in range(comp):
            turned = jnp.zeros((rl, nz), jnp.float32)
            for d in range(3):
                for k in range(comp):
                    turned = turned + jac[d, k, :, c : c + 1] * diffs[d][k]
            out_ref[c, a] = adj[c, a] + step[a] * (0.5 * turned + SMOOTHING * sums[c])

    if few:
        for j in range(1, nc):
            tgt_copies[j - 1].wait_recv()
            build_columns(j, j)

    for c in part_copies:
        c.wait_recv()
    total = part[0]
    for k in range(1, no):
        total = total + part[k]
    src[0] = total
    ps_ref[...] = total
    src_copies = [
        remote(src.at[0], src.at[j], s_send.at[j], s_recv.at[j], (peers_c[j], g))
        for j in range(1, nc)
    ]
    for c in src_copies:
        c.start()

    def land(j, slot, first):
        rad = mod(div(tgt[j], nz), radial_all)
        hits = [rad[t : t + 1, :] == row_id for t in range(tiles)]
        for c in range(comp):
            value = src[j, c]
            high = value.astype(jnp.bfloat16).astype(jnp.float32)
            for p, piece in enumerate((high, value - high)):
                top = (p * comp + c) * rl
                for t in range(tiles):
                    a_buf[slot, top : top + rl, t * tile : (t + 1) * tile] = jnp.where(
                        hits[t], piece[t : t + 1, :], 0.0
                    ).astype(jnp.bfloat16)
        got = lax.dot_general(
            a_buf[slot], bt[j if few else 0], NT, preferred_element_type=jnp.float32
        )
        got = got[: comp * rl] + got[comp * rl :]
        if first:
            acc[...] = got
        else:
            acc[...] += got

    if few:
        land(0, 0, True)
        for j in range(1, nc):
            src_copies[j - 1].wait_recv()
            land(j, j % 2, False)
    else:
        build_columns(0, 0)
        land(0, 0, True)

        def one(j, carry):
            remote(tgt.at[0], tgt.at[j], t_send.at[j], t_recv.at[j], (me, g)).wait_recv()
            remote(src.at[0], src.at[j], s_send.at[j], s_recv.at[j], (me, g)).wait_recv()
            build_columns(j, 0)
            land(j, 0, False)
            return carry

        lax.fori_loop(1, nc, one, 0)

    for c in range(comp):
        for a in range(az):
            out_ref[c, a] += acc[c * rl : (c + 1) * rl, a * nz : (a + 1) * nz]

    for c in part_copies + tgt_copies + az_copies + src_copies:
        c.wait_send()

    @pl.when(has_after)
    def _():
        up.wait_send()

    @pl.when(has_before)
    def _():
        down.wait_send()


def on_device(
    nc, no, histories, amplitude, weights, retarded, owner_block, owner_cell, adjoint, step_size, jacobian
):
    tiles = retarded.shape[1]
    tile = weights.shape[0] // tiles
    comp, az, rl, nz = adjoint.shape
    ob = owner_block.reshape(tiles, tile)
    oc = owner_cell.reshape(tiles, tile)
    args = (
        histories,
        jnp.transpose(amplitude, (1, 0, 2)),
        weights,
        retarded.T,
        ob,
        oc,
        adjoint,
        step_size,
        jnp.transpose(jacobian, (1, 2, 0, 3)),
    )
    slots = nc if nc <= 16 else 1
    f32 = jnp.float32
    dma = pltpu.SemaphoreType.DMA
    out, ps = pl.pallas_call(
        functools.partial(kernel, nc, no),
        out_shape=(
            jax.ShapeDtypeStruct(adjoint.shape, f32),
            jax.ShapeDtypeStruct((comp, tiles, tile), f32),
        ),
        in_specs=[pl.BlockSpec(memory_space=pltpu.HBM)] * len(args),
        out_specs=(pl.BlockSpec(memory_space=pltpu.VMEM),) * 2,
        scratch_shapes=[pltpu.VMEM(x.shape, x.dtype) for x in args]
        + [
            pltpu.VMEM((no, comp, tiles, tile), f32),
            pltpu.VMEM((nc, comp, tiles, tile), f32),
            pltpu.VMEM((nc, tiles, tile), jnp.int32),
            pltpu.VMEM((2, comp, rl, nz), f32),
            pltpu.VMEM((2, comp, az, 8, nz), f32),
            pltpu.VMEM((2, 2 * comp * rl, tiles * tile), jnp.bfloat16),
            pltpu.VMEM((slots, az * nz, tiles * tile), jnp.bfloat16),
            pltpu.VMEM((comp * rl, az * nz), f32),
            dma((len(args),)),
            dma((no,)),
            dma((no,)),
            dma((nc,)),
            dma((nc,)),
            dma((nc,)),
            dma((nc,)),
            dma((4,)),
            dma((4,)),
        ],
        compiler_params=pltpu.CompilerParams(
            collective_id=0, has_side_effects=True, vmem_limit_bytes=67_043_328
        ),
        name="rotor_step",
    )(*args)
    return out, ps.reshape(comp, tiles * tile)


def solution(mesh):
    return jax.shard_map(
        functools.partial(on_device, mesh.shape["cells"], mesh.shape["obs"]),
        mesh=mesh,
        in_specs=(
            P("obs", None),
            P("obs", None, "cells"),
            P("cells", None),
            P("obs", "cells"),
            P("cells"),
            P("cells"),
            P(None, "cells", "obs", None),
            P("cells", "obs", None),
            P("cells", None, None, None),
        ),
        out_specs=(P(None, "cells", "obs", None), P(None, "cells")),
        check_vma=False,
    )
```

```python
import functools

import jax
import jax.numpy as jnp
from jax import lax
from jax.experimental import pallas as pl
from jax.experimental.pallas import tpu as pltpu
from jax.sharding import PartitionSpec as P

MESH = pl.DeviceIdType.MESH
SMOOTHING = 0.25
NT = (((1,), (1,)), ((), ()))


def div(x, d):
    if d & (d - 1) == 0:
        return lax.shift_right_logical(x, jnp.full_like(x, d.bit_length() - 1))
    return lax.div(x, jnp.full_like(x, d))


def mod(x, d):
    if d & (d - 1) == 0:
        return x & (d - 1)
    return lax.rem(x, jnp.full_like(x, d))


def partner(me, j, n):
    if n & (n - 1):
        return lax.rem(me + j, n)
    out = me
    for k in range(n.bit_length() - 1):
        if j >> k & 1:
            out = out + (1 - 2 * ((me // (1 << k)) % 2)) * (1 << k)
    return out


def kernel(
    nc, no,
    hist_h, amp_h, wts_h, ret_h, ob_h, oc_h, adj_h, step_h, jac_h,
    out_ref, ps_ref,
    hist, amp, wts, ret, ob, oc, adj, step, jac,
    part, src, tgt, halo_a, halo_r, edge, a_buf, bt, acc,
    in_sem, ps_send, ps_recv, s_send, s_recv, t_send, t_recv, h_send, h_recv,
):
    me, g = lax.axis_index("cells"), lax.axis_index("obs")
    loads = [
        pltpu.make_async_copy(h, v, in_sem.at[i])
        for i, (h, v) in enumerate(
            [(hist_h, hist), (ret_h, ret), (ob_h, ob), (oc_h, oc), (wts_h, wts), (amp_h, amp),
             (adj_h, adj), (step_h, step), (jac_h, jac)]
        )
    ]
    for c in loads:
        c.start()
    barrier = pltpu.get_barrier_semaphore()
    peers_c = [partner(me, j, nc) for j in range(nc)]
    peers_o = [lax.rem(g + k, no) for k in range(no)]
    for j in range(1, nc):
        pl.semaphore_signal(barrier, inc=1, device_id=(peers_c[j], g), device_id_type=MESH)
    for k in range(1, no):
        pl.semaphore_signal(barrier, inc=1, device_id=(me, peers_o[k]), device_id_type=MESH)

    comp, nobs = amp.shape[0], amp.shape[1]
    samples = wts.shape[1]
    hlen = hist.shape[1]
    tiles = ret.shape[0]
    tile = wts.shape[0] // tiles
    az, rl, nz = adj.shape[1:]
    radial_all = rl * no
    block_cells = az * radial_all * nz

    loads[0].wait()
    loads[1].wait()
    loads[2].wait()
    loads[3].wait()
    tgt[0] = ob[...] * block_cells + oc[...]
    series = hist[...].astype(jnp.float32)
    same = lax.broadcasted_iota(jnp.int32, (nobs, nobs), 0) == lax.broadcasted_iota(
        jnp.int32, (nobs, nobs), 1
    )
    offsets = ret[...].astype(jnp.float32)
    span = hlen - samples
    windows = []
    for t in range(tiles):
        off = jnp.sum(jnp.where(same, offsets[t : t + 1, :], 0.0), axis=1, keepdims=True)
        off = off.astype(jnp.int32)
        x = series
        for bit in reversed(range(span.bit_length())):
            amount = 1 << bit
            moved = pltpu.roll(x, hlen - amount, 1)
            x = jnp.where((off >> bit & 1) == 1, moved, x)
        windows.append(x[:, :samples].astype(jnp.bfloat16))
    loads[6].wait()
    for c in range(comp):
        for a in range(az):
            i = c * az + a
            edge[0, i : i + 1, :] = adj[c, a, rl - 1 : rl, :]
            edge[1, i : i + 1, :] = adj[c, a, 0:1, :]
    loads[4].wait()
    loads[5].wait()
    for t in range(tiles):
        cols = slice(t * tile, (t + 1) * tile)
        proj = lax.dot_general(windows[t], wts[cols, :], NT, preferred_element_type=jnp.float32)
        for c in range(comp):
            product = amp[c, :, cols].astype(jnp.float32) * proj
            part[g, c, t : t + 1, :] = jnp.sum(product, axis=0, keepdims=True)
    pl.semaphore_wait(barrier, nc - 1 + no - 1)

    def remote(s, d, ss, rs, dev):
        return pltpu.make_async_remote_copy(
            src_ref=s, dst_ref=d, send_sem=ss, recv_sem=rs, device_id=dev, device_id_type=MESH
        )

    part_copies = [
        remote(part.at[g], part.at[g], ps_send.at[k], ps_recv.at[k], (me, peers_o[k]))
        for k in range(1, no)
    ]
    for c in part_copies:
        c.start()
    tgt_copies = [
        remote(tgt.at[0], tgt.at[j], t_send.at[j], t_recv.at[j], (peers_c[j], g))
        for j in range(1, nc)
    ]
    for c in tgt_copies:
        c.start()
    after, before = lax.rem(me + 1, nc), lax.rem(me + nc - 1, nc)
    az_copies = [
        remote(adj.at[:, az - 1], halo_a.at[0], h_send.at[0], h_recv.at[0], (after, g)),
        remote(adj.at[:, 0], halo_a.at[1], h_send.at[1], h_recv.at[1], (before, g)),
    ]
    for c in az_copies:
        c.start()
    g_after, g_before = lax.rem(g + 1, no), lax.rem(g + no - 1, no)
    up = remote(edge.at[0], halo_r.at[0], h_send.at[2], h_recv.at[2], (me, g_after))
    down = remote(edge.at[1], halo_r.at[1], h_send.at[3], h_recv.at[3], (me, g_before))
    has_after, has_before = g < no - 1, g > 0

    @pl.when(has_after)
    def _():
        up.start()

    @pl.when(has_before)
    def _():
        down.start()

    column_id = lax.broadcasted_iota(jnp.int32, (az * nz, tile), 0) + me * (az * nz)
    row_id = lax.broadcasted_iota(jnp.int32, (rl, tile), 0) + g * rl

    def build_columns(j, slot):
        flat = tgt[j]
        code = div(flat, radial_all * nz) * nz + mod(flat, nz)
        for t in range(tiles):
            hit = code[t : t + 1, :] == column_id
            bt[slot, :, t * tile : (t + 1) * tile] = jnp.where(hit, 1.0, 0.0).astype(jnp.bfloat16)

    few = bt.shape[0] == nc
    if few:
        build_columns(0, 0)

    if few:
        for j in range(1, nc):
            tgt_copies[j - 1].wait_recv()
            build_columns(j, j)

    for c in part_copies:
        c.wait_recv()
    total = part[0]
    for k in range(1, no):
        total = total + part[k]
    src[0] = total
    ps_ref[...] = total
    src_copies = [
        remote(src.at[0], src.at[j], s_send.at[j], s_recv.at[j], (peers_c[j], g))
        for j in range(1, nc)
    ]
    for c in src_copies:
        c.start()

    def land(j, slot, first):
        rad = mod(div(tgt[j], nz), radial_all)
        hits = [rad[t : t + 1, :] == row_id for t in range(tiles)]
        for c in range(comp):
            value = src[j, c]
            high = value.astype(jnp.bfloat16).astype(jnp.float32)
            for p, piece in enumerate((high, value - high)):
                top = (p * comp + c) * rl
                for t in range(tiles):
                    a_buf[slot, top : top + rl, t * tile : (t + 1) * tile] = jnp.where(
                        hits[t], piece[t : t + 1, :], 0.0
                    ).astype(jnp.bfloat16)
        got = lax.dot_general(
            a_buf[slot], bt[j if few else 0], NT, preferred_element_type=jnp.float32
        )
        got = got[: comp * rl] + got[comp * rl :]
        if first:
            acc[...] = got
        else:
            acc[...] += got

    loads[7].wait()
    loads[8].wait()
    for c in az_copies:
        c.wait_recv()

    @pl.when(has_before)
    def _():
        up.wait_recv()

    @pl.when(has_after)
    def _():
        down.wait_recv()

    @pl.when(jnp.logical_not(has_before))
    def _():
        halo_r[0] = jnp.zeros(halo_r.shape[1:], jnp.float32)

    @pl.when(jnp.logical_not(has_after))
    def _():
        halo_r[1] = jnp.zeros(halo_r.shape[1:], jnp.float32)

    row = lax.broadcasted_iota(jnp.int32, (rl, nz), 0)
    lane = lax.broadcasted_iota(jnp.int32, (rl, nz), 1)
    for a in range(az):
        diffs = [[], [], []]
        sums = []
        for c in range(comp):
            x = adj[c, a]
            f0 = adj[c, a + 1] if a + 1 < az else halo_a[1, c]
            b0 = adj[c, a - 1] if a > 0 else halo_a[0, c]
            f1 = jnp.where(row == rl - 1, halo_r[1, c * az + a : c * az + a + 1, :], pltpu.roll(x, rl - 1, 0))
            b1 = jnp.where(row == 0, halo_r[0, c * az + a : c * az + a + 1, :], pltpu.roll(x, 1, 0))
            f2 = jnp.where(lane == nz - 1, 0.0, pltpu.roll(x, nz - 1, 1))
            b2 = jnp.where(lane == 0, 0.0, pltpu.roll(x, 1, 1))
            diffs[0].append(f0 - b0)
            diffs[1].append(f1 - b1)
            diffs[2].append(f2 - b2)
            sums.append(((f0 + b0) + (f1 + b1)) + (f2 + b2) - 6.0 * x)
        for c in range(comp):
            turned = jnp.zeros((rl, nz), jnp.float32)
            for d in range(3):
                for k in range(comp):
                    turned = turned + jac[d, k, :, c : c + 1] * diffs[d][k]
            out_ref[c, a] = adj[c, a] + step[a] * (0.5 * turned + SMOOTHING * sums[c])

    if few:
        land(0, 0, True)
        for j in range(1, nc):
            src_copies[j - 1].wait_recv()
            land(j, j % 2, False)
    else:
        build_columns(0, 0)
        land(0, 0, True)

        def one(j, carry):
            remote(tgt.at[0], tgt.at[j], t_send.at[j], t_recv.at[j], (me, g)).wait_recv()
            remote(src.at[0], src.at[j], s_send.at[j], s_recv.at[j], (me, g)).wait_recv()
            build_columns(j, 0)
            land(j, 0, False)
            return carry

        lax.fori_loop(1, nc, one, 0)

    for c in range(comp):
        for a in range(az):
            out_ref[c, a] += acc[c * rl : (c + 1) * rl, a * nz : (a + 1) * nz]

    for c in part_copies + tgt_copies + az_copies + src_copies:
        c.wait_send()

    @pl.when(has_after)
    def _():
        up.wait_send()

    @pl.when(has_before)
    def _():
        down.wait_send()


def on_device(
    nc, no, histories, amplitude, weights, retarded, owner_block, owner_cell, adjoint, step_size, jacobian
):
    tiles = retarded.shape[1]
    tile = weights.shape[0] // tiles
    comp, az, rl, nz = adjoint.shape
    ob = owner_block.reshape(tiles, tile)
    oc = owner_cell.reshape(tiles, tile)
    args = (
        histories,
        jnp.transpose(amplitude, (1, 0, 2)),
        weights,
        retarded.T,
        ob,
        oc,
        adjoint,
        step_size,
        jnp.transpose(jacobian, (1, 2, 0, 3)),
    )
    slots = nc if nc <= 16 else 1
    f32 = jnp.float32
    dma = pltpu.SemaphoreType.DMA
    out, ps = pl.pallas_call(
        functools.partial(kernel, nc, no),
        out_shape=(
            pltpu.VMEM(adjoint.shape, f32),
            pltpu.VMEM((comp, tiles, tile), f32),
        ),
        in_specs=[pl.BlockSpec(memory_space=pltpu.HBM)] * len(args),
        out_specs=(pl.BlockSpec(memory_space=pltpu.VMEM),) * 2,
        scratch_shapes=[pltpu.VMEM(x.shape, x.dtype) for x in args]
        + [
            pltpu.VMEM((no, comp, tiles, tile), f32),
            pltpu.VMEM((nc, comp, tiles, tile), f32),
            pltpu.VMEM((nc, tiles, tile), jnp.int32),
            pltpu.VMEM((2, comp, rl, nz), f32),
            pltpu.VMEM((2, comp * az, nz), f32),
            pltpu.VMEM((2, comp * az, nz), f32),
            pltpu.VMEM((2, 2 * comp * rl, tiles * tile), jnp.bfloat16),
            pltpu.VMEM((slots, az * nz, tiles * tile), jnp.bfloat16),
            pltpu.VMEM((comp * rl, az * nz), f32),
            dma((len(args),)),
            dma((no,)),
            dma((no,)),
            dma((nc,)),
            dma((nc,)),
            dma((nc,)),
            dma((nc,)),
            dma((4,)),
            dma((4,)),
        ],
        compiler_params=pltpu.CompilerParams(
            collective_id=0, has_side_effects=True, vmem_limit_bytes=67_043_328 - 120_000
        ),
        name="rotor_step",
    )(*args)
    return out, ps.reshape(comp, tiles * tile)


def solution(mesh):
    return jax.shard_map(
        functools.partial(on_device, mesh.shape["cells"], mesh.shape["obs"]),
        mesh=mesh,
        in_specs=(
            P("obs", None),
            P("obs", None, "cells"),
            P("cells", None),
            P("obs", "cells"),
            P("cells"),
            P("cells"),
            P(None, "cells", "obs", None),
            P("cells", "obs", None),
            P("cells", None, None, None),
        ),
        out_specs=(P(None, "cells", "obs", None), P(None, "cells")),
        check_vma=False,
    )
```

```python
import functools

import jax
import jax.numpy as jnp
from jax import lax
from jax.experimental import pallas as pl
from jax.experimental.pallas import tpu as pltpu
from jax.sharding import PartitionSpec as P

MESH = pl.DeviceIdType.MESH
SMOOTHING = 0.25
NT = (((1,), (1,)), ((), ()))


def div(x, d):
    if d & (d - 1) == 0:
        return lax.shift_right_logical(x, jnp.full_like(x, d.bit_length() - 1))
    return lax.div(x, jnp.full_like(x, d))


def mod(x, d):
    if d & (d - 1) == 0:
        return x & (d - 1)
    return lax.rem(x, jnp.full_like(x, d))


def partner(me, j, n):
    if n & (n - 1):
        return lax.rem(me + j, n)
    out = me
    for k in range(n.bit_length() - 1):
        if j >> k & 1:
            out = out + (1 - 2 * ((me // (1 << k)) % 2)) * (1 << k)
    return out


def kernel(
    nc, no,
    hist_h, amp_h, wts_h, ret_h, ob_h, oc_h, adj_h, step_h, jac_h,
    out_ref, ps_ref,
    hist, amp, wts, ret, ob, oc, adj, step, jac,
    part, src, tgt, halo_a, halo_r, edge, a_buf, bt, acc,
    in_sem, ps_send, ps_recv, s_send, s_recv, t_send, t_recv, h_send, h_recv,
):
    me, g = lax.axis_index("cells"), lax.axis_index("obs")
    loads = [
        pltpu.make_async_copy(h, v, in_sem.at[i])
        for i, (h, v) in enumerate(
            [(hist_h, hist), (ret_h, ret), (ob_h, ob), (oc_h, oc), (wts_h, wts), (amp_h, amp),
             (adj_h, adj), (step_h, step), (jac_h, jac)]
        )
    ]
    for c in loads:
        c.start()
    barrier = pltpu.get_barrier_semaphore()
    peers_c = [partner(me, j, nc) for j in range(nc)]
    peers_o = [lax.rem(g + k, no) for k in range(no)]
    for j in range(1, nc):
        pl.semaphore_signal(barrier, inc=1, device_id=(peers_c[j], g), device_id_type=MESH)
    for k in range(1, no):
        pl.semaphore_signal(barrier, inc=1, device_id=(me, peers_o[k]), device_id_type=MESH)

    comp, nobs = amp.shape[0], amp.shape[1]
    samples = wts.shape[1]
    hlen = hist.shape[1]
    tiles = ret.shape[0]
    tile = wts.shape[0] // tiles
    az, rl, nz = adj.shape[1:]
    radial_all = rl * no
    block_cells = az * radial_all * nz

    loads[0].wait()
    loads[1].wait()
    loads[2].wait()
    loads[3].wait()
    tgt[0] = ob[...] * block_cells + oc[...]
    series = hist[...].astype(jnp.float32)
    same = lax.broadcasted_iota(jnp.int32, (nobs, nobs), 0) == lax.broadcasted_iota(
        jnp.int32, (nobs, nobs), 1
    )
    offsets = ret[...].astype(jnp.float32)
    span = hlen - samples
    windows = []
    for t in range(tiles):
        off = jnp.sum(jnp.where(same, offsets[t : t + 1, :], 0.0), axis=1, keepdims=True)
        off = off.astype(jnp.int32)
        x = series
        for bit in reversed(range(span.bit_length())):
            amount = 1 << bit
            moved = pltpu.roll(x, hlen - amount, 1)
            x = jnp.where((off >> bit & 1) == 1, moved, x)
        windows.append(x[:, :samples].astype(jnp.bfloat16))
    loads[6].wait()
    for c in range(comp):
        for a in range(az):
            i = c * az + a
            edge[0, i : i + 1, :] = adj[c, a, rl - 1 : rl, :]
            edge[1, i : i + 1, :] = adj[c, a, 0:1, :]
    loads[4].wait()
    loads[5].wait()
    for t in range(tiles):
        cols = slice(t * tile, (t + 1) * tile)
        proj = lax.dot_general(windows[t], wts[cols, :], NT, preferred_element_type=jnp.float32)
        for c in range(comp):
            product = amp[c, :, cols].astype(jnp.float32) * proj
            part[g, c, t : t + 1, :] = jnp.sum(product, axis=0, keepdims=True)
    column_id = lax.broadcasted_iota(jnp.int32, (az * nz, tile), 0) + me * (az * nz)
    row_id = lax.broadcasted_iota(jnp.int32, (rl, tile), 0) + g * rl

    def build_columns(j, slot):
        flat = tgt[j]
        code = div(flat, radial_all * nz) * nz + mod(flat, nz)
        for t in range(tiles):
            hit = code[t : t + 1, :] == column_id
            bt[slot, :, t * tile : (t + 1) * tile] = jnp.where(hit, 1.0, 0.0).astype(jnp.bfloat16)

    few = bt.shape[0] == nc
    if few:
        build_columns(0, 0)

    pl.semaphore_wait(barrier, nc - 1 + no - 1)

    def remote(s, d, ss, rs, dev):
        return pltpu.make_async_remote_copy(
            src_ref=s, dst_ref=d, send_sem=ss, recv_sem=rs, device_id=dev, device_id_type=MESH
        )

    part_copies = [
        remote(part.at[g], part.at[g], ps_send.at[k], ps_recv.at[k], (me, peers_o[k]))
        for k in range(1, no)
    ]
    for c in part_copies:
        c.start()
    tgt_copies = [
        remote(tgt.at[0], tgt.at[j], t_send.at[j], t_recv.at[j], (peers_c[j], g))
        for j in range(1, nc)
    ]
    for c in tgt_copies:
        c.start()
    after, before = lax.rem(me + 1, nc), lax.rem(me + nc - 1, nc)
    az_copies = [
        remote(adj.at[:, az - 1], halo_a.at[0], h_send.at[0], h_recv.at[0], (after, g)),
        remote(adj.at[:, 0], halo_a.at[1], h_send.at[1], h_recv.at[1], (before, g)),
    ]
    for c in az_copies:
        c.start()
    g_after, g_before = lax.rem(g + 1, no), lax.rem(g + no - 1, no)
    up = remote(edge.at[0], halo_r.at[0], h_send.at[2], h_recv.at[2], (me, g_after))
    down = remote(edge.at[1], halo_r.at[1], h_send.at[3], h_recv.at[3], (me, g_before))
    has_after, has_before = g < no - 1, g > 0

    @pl.when(has_after)
    def _():
        up.start()

    @pl.when(has_before)
    def _():
        down.start()

    if few:
        for j in range(1, nc // 2):
            tgt_copies[j - 1].wait_recv()
            build_columns(j, j)

    for c in part_copies:
        c.wait_recv()
    total = part[0]
    for k in range(1, no):
        total = total + part[k]
    src[0] = total
    ps_ref[...] = total
    src_copies = [
        remote(src.at[0], src.at[j], s_send.at[j], s_recv.at[j], (peers_c[j], g))
        for j in range(1, nc)
    ]
    for c in src_copies:
        c.start()

    def land(j, slot, first):
        rad = mod(div(tgt[j], nz), radial_all)
        hits = [rad[t : t + 1, :] == row_id for t in range(tiles)]
        for c in range(comp):
            value = src[j, c]
            high = value.astype(jnp.bfloat16).astype(jnp.float32)
            for p, piece in enumerate((high, value - high)):
                top = (p * comp + c) * rl
                for t in range(tiles):
                    a_buf[slot, top : top + rl, t * tile : (t + 1) * tile] = jnp.where(
                        hits[t], piece[t : t + 1, :], 0.0
                    ).astype(jnp.bfloat16)
        got = lax.dot_general(
            a_buf[slot], bt[j if few else 0], NT, preferred_element_type=jnp.float32
        )
        got = got[: comp * rl] + got[comp * rl :]
        if first:
            acc[...] = got
        else:
            acc[...] += got

    loads[7].wait()
    loads[8].wait()
    for c in az_copies:
        c.wait_recv()

    @pl.when(has_before)
    def _():
        up.wait_recv()

    @pl.when(has_after)
    def _():
        down.wait_recv()

    @pl.when(jnp.logical_not(has_before))
    def _():
        halo_r[0] = jnp.zeros(halo_r.shape[1:], jnp.float32)

    @pl.when(jnp.logical_not(has_after))
    def _():
        halo_r[1] = jnp.zeros(halo_r.shape[1:], jnp.float32)

    row = lax.broadcasted_iota(jnp.int32, (rl, nz), 0)
    lane = lax.broadcasted_iota(jnp.int32, (rl, nz), 1)
    for a in range(az):
        diffs = [[], [], []]
        sums = []
        for c in range(comp):
            x = adj[c, a]
            f0 = adj[c, a + 1] if a + 1 < az else halo_a[1, c]
            b0 = adj[c, a - 1] if a > 0 else halo_a[0, c]
            f1 = jnp.where(row == rl - 1, halo_r[1, c * az + a : c * az + a + 1, :], pltpu.roll(x, rl - 1, 0))
            b1 = jnp.where(row == 0, halo_r[0, c * az + a : c * az + a + 1, :], pltpu.roll(x, 1, 0))
            f2 = jnp.where(lane == nz - 1, 0.0, pltpu.roll(x, nz - 1, 1))
            b2 = jnp.where(lane == 0, 0.0, pltpu.roll(x, 1, 1))
            diffs[0].append(f0 - b0)
            diffs[1].append(f1 - b1)
            diffs[2].append(f2 - b2)
            sums.append(((f0 + b0) + (f1 + b1)) + (f2 + b2) - 6.0 * x)
        for c in range(comp):
            turned = jnp.zeros((rl, nz), jnp.float32)
            for d in range(3):
                for k in range(comp):
                    turned = turned + jac[d, k, :, c : c + 1] * diffs[d][k]
            out_ref[c, a] = adj[c, a] + step[a] * (0.5 * turned + SMOOTHING * sums[c])

    if few:
        land(0, 0, True)
        for j in range(1, nc):
            if j == 1:
                for i in range(nc // 2, nc):
                    tgt_copies[i - 1].wait_recv()
                    build_columns(i, i)
            src_copies[j - 1].wait_recv()
            land(j, j % 2, False)
    else:
        build_columns(0, 0)
        land(0, 0, True)

        def one(j, carry):
            remote(tgt.at[0], tgt.at[j], t_send.at[j], t_recv.at[j], (me, g)).wait_recv()
            remote(src.at[0], src.at[j], s_send.at[j], s_recv.at[j], (me, g)).wait_recv()
            build_columns(j, 0)
            land(j, 0, False)
            return carry

        lax.fori_loop(1, nc, one, 0)

    for c in range(comp):
        for a in range(az):
            out_ref[c, a] += acc[c * rl : (c + 1) * rl, a * nz : (a + 1) * nz]

    for c in part_copies + tgt_copies + az_copies + src_copies:
        c.wait_send()

    @pl.when(has_after)
    def _():
        up.wait_send()

    @pl.when(has_before)
    def _():
        down.wait_send()


def on_device(
    nc, no, histories, amplitude, weights, retarded, owner_block, owner_cell, adjoint, step_size, jacobian
):
    tiles = retarded.shape[1]
    tile = weights.shape[0] // tiles
    comp, az, rl, nz = adjoint.shape
    ob = owner_block.reshape(tiles, tile)
    oc = owner_cell.reshape(tiles, tile)
    args = (
        histories,
        jnp.transpose(amplitude, (1, 0, 2)),
        weights,
        retarded.T,
        ob,
        oc,
        adjoint,
        step_size,
        jnp.transpose(jacobian, (1, 2, 0, 3)),
    )
    slots = nc if nc <= 16 else 1
    f32 = jnp.float32
    dma = pltpu.SemaphoreType.DMA
    out, ps = pl.pallas_call(
        functools.partial(kernel, nc, no),
        out_shape=(
            pltpu.VMEM(adjoint.shape, f32),
            pltpu.VMEM((comp, tiles, tile), f32),
        ),
        in_specs=[pl.BlockSpec(memory_space=pltpu.HBM)] * len(args),
        out_specs=(pl.BlockSpec(memory_space=pltpu.VMEM),) * 2,
        scratch_shapes=[pltpu.VMEM(x.shape, x.dtype) for x in args]
        + [
            pltpu.VMEM((no, comp, tiles, tile), f32),
            pltpu.VMEM((nc, comp, tiles, tile), f32),
            pltpu.VMEM((nc, tiles, tile), jnp.int32),
            pltpu.VMEM((2, comp, rl, nz), f32),
            pltpu.VMEM((2, comp * az, nz), f32),
            pltpu.VMEM((2, comp * az, nz), f32),
            pltpu.VMEM((2, 2 * comp * rl, tiles * tile), jnp.bfloat16),
            pltpu.VMEM((slots, az * nz, tiles * tile), jnp.bfloat16),
            pltpu.VMEM((comp * rl, az * nz), f32),
            dma((len(args),)),
            dma((no,)),
            dma((no,)),
            dma((nc,)),
            dma((nc,)),
            dma((nc,)),
            dma((nc,)),
            dma((4,)),
            dma((4,)),
        ],
        compiler_params=pltpu.CompilerParams(
            collective_id=0, has_side_effects=True, vmem_limit_bytes=67_043_328 - 120_000
        ),
        name="rotor_step",
    )(*args)
    return out, ps.reshape(comp, tiles * tile)


def solution(mesh):
    return jax.shard_map(
        functools.partial(on_device, mesh.shape["cells"], mesh.shape["obs"]),
        mesh=mesh,
        in_specs=(
            P("obs", None),
            P("obs", None, "cells"),
            P("cells", None),
            P("obs", "cells"),
            P("cells"),
            P("cells"),
            P(None, "cells", "obs", None),
            P("cells", "obs", None),
            P("cells", None, None, None),
        ),
        out_specs=(P(None, "cells", "obs", None), P(None, "cells")),
        check_vma=False,
    )
```
